256 devices in a mesh: ctx: 64 (over y, z, core), head: 4 (over x).
Axes of the slice: x: 4, y: 4, z: 8, core: 2. Of those that a mesh axis runs over, the one named last changes fastest.
Arguments:
- query: bfloat16 [8192, 32, 128], P('ctx', 'head'), may hold values from -6 to 6
- key: bfloat16 [8192, 4, 128], P(('ctx', 'head')), may hold values from -6 to 6
- value: bfloat16 [8192, 4, 128], P(('ctx', 'head')), may hold values from -6 to 6
- d_out: bfloat16 [8192, 32, 128], P('ctx', 'head'), may hold values from -6 to 6
- seg_blocks: int32 [32], replicated, may hold values from 1 to 4, 64 in all
- seg_audio: int32 [32], replicated, may hold values 0 or 1
Outputs:
- d_query: bfloat16 [8192, 32, 128], P('ctx', 'head')
- d_key: bfloat16 [8192, 4, 128], P(('ctx', 'head'))
- d_value: bfloat16 [8192, 4, 128], P(('ctx', 'head'))
The draws below stay inside these ranges and needn't reach their ends.
Inputs may be any that keep to these rules, and one draw needn't show every extreme that they name: `seg_blocks`: the segments tile the 64 blocks in order: their lengths sum to 64.
All inputs are finite; a program needn't handle non-finite values.
Results may differ from the reference program's by a relative error of at most 0.0055.
Values may be sent and summed in bfloat16 or wider, within the bound.
No kernel may reach another device: no remote copies, remote signals or barrier semaphores. Data moves between devices by JAX's collectives and lax.ppermute only.
A program may use at most 128 MiB of HBM per device.

```python
import math
import jax
import jax.numpy as jnp
import numpy as np
from jax import lax

DH = 128
GROUP = 8
KVH = 4
HQ = 32
BLK = 128
MOST = 4
L = 8192
NB = 64
NSEG = 32


def draw_query(key, part):
    entries = jax.random.truncated_normal(jax.random.fold_in(key, 3), -6.0, 6.0, (L, HQ, DH), jnp.float32)
    return entries.astype(jnp.bfloat16)


def draw_key(key, part):
    entries = jax.random.truncated_normal(jax.random.fold_in(key, 5), -6.0, 6.0, (L, KVH, DH), jnp.float32)
    return entries.astype(jnp.bfloat16)


def plant(values, rng, smallest, top_value):
    index_at = [jax.random.randint(jax.random.fold_in(rng, axis), (), 0, length) for axis, length in enumerate(values.shape)]
    main_axis = values.shape.index(max(values.shape))
    next_to = index_at[:main_axis] + [(index_at[main_axis] + 1) % values.shape[main_axis]] + index_at[main_axis + 1:]
    return values.at[tuple(index_at)].set(smallest).at[tuple(next_to)].set(top_value)


def block_scale(key, extent, split, low, high):
    gain, own = 1.0, jax.random.fold_in(key, 6)
    for dim, shards_of in split:
        heights = jnp.exp(jax.random.uniform(jax.random.fold_in(own, dim), (shards_of,), jnp.float32, low / len(split), high / len(split)))
        gain = gain * jnp.repeat(heights, extent[dim] // shards_of).reshape([-1 if axis == dim else 1 for axis in range(len(extent))])
    return gain


def split_up(count, total, bound, skew):
    weights = [(1 << 20) // math.isqrt(rank ** skew) + 1 for rank in range(2, count + 1)]
    surplus, given = total - bound - (count - 1), [1] * (count - 1)
    while surplus > 0:
        free = [i for i in range(count - 1) if given[i] < bound]
        whole, budget = sum([weights[i] for i in free]), surplus
        for i in free:
            addition = min(bound - given[i], max(1, budget * weights[i] // whole), surplus)
            given[i] = given[i] + addition
            surplus = surplus - addition
    return np.array([bound] + given)


def uneven_parts(own_key, number_of, total, reach, slope):
    if number_of == 2:
        one = jax.random.randint(own_key, (), max(1, total - reach), min(reach, total - 1) + 1)
        return jnp.stack([one, total - one])
    tallies = jnp.asarray(split_up(number_of, total, reach, slope), jnp.int32)
    couples = (number_of - 1) // 2
    giver, sink = tallies[1:1 + 2 * couples:2], tallies[2:2 + 2 * couples:2]
    room = jnp.minimum(giver - 1, reach - sink)
    moved = jax.random.randint(jax.random.fold_in(own_key, 1), (couples,), 0, 1 << 20) % (room + 1)
    tallies = tallies.at[1:1 + 2 * couples:2].set(giver - moved).at[2:2 + 2 * couples:2].set(sink + moved)
    return tallies[jax.random.permutation(jax.random.fold_in(own_key, 2), number_of)]


def bell_draw(stream_key, dims, width, most, pieces=(), kind=jnp.bfloat16):
    values = jax.random.normal(stream_key, dims, jnp.float32) * width
    if len(pieces) > 0:
        values = block_scale(stream_key, dims, pieces, -0.22, 0.18) * values
    return jnp.clip(values, min=-most, max=most).astype(kind)


def setup_inputs(seed: int = 0) -> dict:
    splits = jax.random.split(jax.random.key(seed), 7)
    return {
        "query": draw_query(jax.random.fold_in(splits[6], 71), 0),
        "key": draw_key(jax.random.fold_in(splits[6], 71), 0),
        "value": bell_draw(splits[2], (L, KVH, DH), 1.0, 6.0, ((0, 256),)),
        "d_out": bell_draw(splits[3], (L, HQ, DH), 1.0, 6.0, ((0, 64), (1, 4))),
        "seg_blocks": uneven_parts(splits[4], NSEG, NB, MOST, 1).astype(jnp.int32),
        "seg_audio": plant((jax.random.randint(splits[5], (NSEG,), 0, 2) < 1).astype(jnp.int32), jax.random.fold_in(splits[5], 1), 0, 1),
    }


NEG = -1e+30

def segment_tables(seg_blocks, seg_audio, positions):
    ends = jnp.cumsum(seg_blocks).astype(jnp.int32)
    starts = (ends - seg_blocks).astype(jnp.int32)
    blocks = (positions // BLK).astype(jnp.int32)
    inside = (starts[None, :] <= blocks[:, None]) & (blocks[:, None] < ends[None, :])
    numbers = jnp.arange(seg_blocks.shape[0], dtype=jnp.int32)
    segment = lax.optimization_barrier(jnp.sum(jnp.where(inside, numbers[None, :], 0), axis=1)).astype(jnp.int32)
    audio = lax.optimization_barrier(jnp.sum(jnp.where(inside, seg_audio[None, :], 0), axis=1)).astype(jnp.int32)
    return (segment, audio)

def visible(query_pos, key_pos, query_seg, query_audio, key_seg):
    causal = key_pos[None, :] <= query_pos[:, None]
    span = (query_seg[:, None] == key_seg[None, :]) & (query_audio[:, None] == 1)
    return causal | span

def reference(query, key, value, d_out, seg_blocks, seg_audio):
    total = query.shape[0]
    count = total // BLK
    scale = 1.0 / math.sqrt(DH)
    positions = jnp.arange(total, dtype=jnp.int32)
    segment, audio = segment_tables(seg_blocks, seg_audio, positions)
    grads_query, grads_key, grads_value = ([], [], [])
    for group_head in range(KVH):
        keys = key[:, group_head, :]
        values = value[:, group_head, :]
        lower = group_head * GROUP
        query_blocks = query[:, lower:lower + GROUP, :].reshape(count, BLK * GROUP, DH)
        out_blocks = d_out[:, lower:lower + GROUP, :].reshape(count, BLK * GROUP, DH)
        inputs = (query_blocks, out_blocks, positions.reshape(count, BLK), segment.reshape(count, BLK), audio.reshape(count, BLK))

        def step(carry, block_inputs):
            key_grad, value_grad = carry
            query_rows, out_rows, query_pos, query_seg, query_audio = block_inputs
            mask = visible(query_pos, positions, query_seg, query_audio, segment)[:, None, :]
            scores = (jnp.dot(query_rows, keys.T, preferred_element_type=jnp.float32) * scale).reshape(BLK, GROUP, total)
            highest = lax.optimization_barrier(jnp.max(jnp.where(mask, scores, NEG), axis=2, keepdims=True))
            lse = highest + jnp.log(lax.optimization_barrier(jnp.sum(jnp.where(mask, jnp.exp(scores - highest), 0.0), axis=2, keepdims=True)))
            probs = jnp.where(mask, jnp.exp(scores - lse), 0.0)
            d_probs = jnp.dot(out_rows, values.T, preferred_element_type=jnp.float32).reshape(BLK, GROUP, total)
            delta = lax.optimization_barrier(jnp.sum(probs * d_probs, axis=2, keepdims=True))
            probs_low = probs.astype(jnp.bfloat16).reshape(BLK * GROUP, total)
            d_scores = (probs * (d_probs - delta)).astype(jnp.bfloat16).reshape(BLK * GROUP, total)
            value_grad = value_grad + jnp.dot(probs_low.T, out_rows, preferred_element_type=jnp.float32)
            key_grad = key_grad + jnp.dot(d_scores.T, query_rows, preferred_element_type=jnp.float32)
            grad_rows = (jnp.dot(d_scores, keys, preferred_element_type=jnp.float32) * scale).astype(jnp.bfloat16)
            return ((key_grad, value_grad), grad_rows)
        zeros = jnp.zeros((total, DH), jnp.float32)
        (key_grad, value_grad), grad_rows = lax.scan(step, (zeros, zeros), inputs)
        grads_query.append(grad_rows.reshape(total, GROUP, DH))
        grads_key.append((key_grad * scale).astype(jnp.bfloat16))
        grads_value.append(value_grad.astype(jnp.bfloat16))
    return (jnp.concatenate(grads_query, axis=1), jnp.stack(grads_key, axis=1), jnp.stack(grads_value, axis=1))
```

```python
import math

import jax
import jax.numpy as jnp
from jax import lax
from jax.experimental import pallas as pl
from jax.experimental.pallas import tpu as pltpu
from jax.sharding import Mesh, PartitionSpec as P

DH = 128
GROUP = 8
BLK = 128
NY, NZ, NC, NX = 4, 8, 2, 4
NSEG = 32
ROWS = BLK * GROUP
SLICE = BLK // NY
COL = NZ * NC * SLICE
NEG = -1e30
SCALE = 1.0 / math.sqrt(DH)
SCALE2 = SCALE * math.log2(math.e)
RB = 512
CROSS = 4 * SLICE
BF, F32 = jnp.bfloat16, jnp.float32
VM = pl.BlockSpec(memory_space=pltpu.VMEM)
SM = pl.BlockSpec(memory_space=pltpu.SMEM)
HB = pl.BlockSpec(memory_space=pl.ANY)


def dot_nt(a, b):
    return lax.dot_general(a, b, (((1,), (1,)), ((), ())), preferred_element_type=F32)


def dot_nn(a, b):
    return lax.dot_general(a, b, (((1,), (0,)), ((), ())), preferred_element_type=F32)


def dot_tn(a, b):
    return lax.dot_general(a, b, (((0,), (0,)), ((), ())), preferred_element_type=F32)


def span_ends(where, seg_blocks, seg_audio):
    blocks = [i * NZ * NC + where[1] * NC + where[2] for i in range(NY)]

    def step(s, carry):
        start, found = carry
        end = start + seg_blocks[s]
        value = jnp.where(seg_audio[s] == 1, end * BLK, 0)
        found = tuple(
            jnp.where((start <= b) & (b < end), value, f) for b, f in zip(blocks, found)
        )
        return (end, found)

    zero = jnp.int32(0)
    return lax.fori_loop(0, NSEG, step, (zero, (zero,) * NY))[1]


def pick(i, values):
    out = values[0]
    for n in range(1, len(values)):
        out = jnp.where(i == n, values[n], out)
    return out


def load_all(where, q_refs, o_refs, z_ref, c_ref, q_buf, o_buf, kv_buf, sem):
    y, z, c, x = (where[n] for n in range(4))
    copies = []
    for d in range(NY):
        i = lax.rem(y + d, NY)
        copies.append(pltpu.make_async_copy(q_refs[d], q_buf.at[i], sem.at[0]))
        copies.append(pltpu.make_async_copy(o_refs[d], o_buf.at[i], sem.at[0]))
    for e, ref in enumerate((z_ref, c_ref)):
        for d in range(NZ):
            block = lax.rem(z + NZ - d, NZ) * NC + (c if e == 0 else 1 - c)
            for r in range(NX):
                j = lax.rem(x + NX - r, NX)
                copies.append(
                    pltpu.make_async_copy(ref.at[d, r], kv_buf.at[:, j, block], sem.at[0])
                )
    for copy in copies:
        copy.start()
    for copy in copies:
        copy.wait()


def visible(where, ends, j, i, count, rows_from, rows):
    n = lax.broadcasted_iota(jnp.int32, (count, 1), 0)
    key_pos = (j * NZ * NC + n // SLICE) * BLK + where[0] * SLICE + n % SLICE
    r = lax.broadcasted_iota(jnp.int32, (1, rows), 1) + rows_from
    query_pos = (i * NZ * NC + where[1] * NC + where[2]) * BLK + r // GROUP
    return key_pos < jnp.maximum(query_pos + 1, pick(i, ends))


def each_pair(ends, pair):
    def full(p, carry):
        i = 1 + (p >= 1).astype(jnp.int32) + (p >= 3).astype(jnp.int32)
        pair(p - i * (i - 1) // 2, i, COL, False)
        return carry

    def diagonal(i, carry):
        pair(i, i, COL, True)
        return carry

    def crossing(i, carry):
        @pl.when(pick(i, ends) > (i + 1) * NZ * NC * BLK)
        def _():
            pair(i + 1, i, CROSS, True)

        return carry

    lax.fori_loop(0, NY, diagonal, 0)
    lax.fori_loop(0, NY * (NY - 1) // 2, full, 0)
    lax.fori_loop(0, NY - 1, crossing, 0)


def stats_kernel(where, seg_blocks, seg_audio, *refs):
    q_refs, o_refs = refs[:NY], refs[NY : 2 * NY]
    z_ref, c_ref, out, q_buf, o_buf, kv_buf, high, total, weighted, sem = refs[2 * NY :]
    load_all(where, q_refs, o_refs, z_ref, c_ref, q_buf, o_buf, kv_buf, sem)
    ends = span_ends(where, seg_blocks, seg_audio)
    high[...] = jnp.full_like(high, NEG)
    total[...] = jnp.zeros_like(total)
    weighted[...] = jnp.zeros_like(weighted)

    def pair(j, i, count, masked):
        k = kv_buf[0, j].reshape(COL, DH)[:count]
        v = kv_buf[1, j].reshape(COL, DH)[:count]
        for r in range(0, ROWS, RB):
            rows = slice(r, r + RB)
            s = dot_nt(k, q_buf[i, rows, :]) * SCALE2
            if masked:
                seen = visible(where, ends, j, i, count, r, RB)
                s = jnp.where(seen, s, NEG)
            dp = dot_nt(v, o_buf[i, rows, :]).reshape(count // 8, 8, RB)
            s = s.reshape(count // 8, 8, RB)
            old = high[i, :, rows]
            new = jnp.maximum(old, jnp.max(s, axis=0))
            fix = jnp.exp2(old - new)
            p = jnp.exp2(s - new[None])
            if masked:
                p = jnp.where(seen.reshape(count // 8, 8, RB), p, 0.0)
            high[i, :, rows] = new
            total[i, :, rows] = total[i, :, rows] * fix + jnp.sum(p, axis=0)
            weighted[i, :, rows] = weighted[i, :, rows] * fix + jnp.sum(p * dp, axis=0)

    each_pair(ends, pair)
    top = jnp.max(high[...], axis=1, keepdims=True)
    fix = jnp.exp2(high[...] - top)
    out[:, 0:1, :] = top
    out[:, 1:2, :] = jnp.sum(total[...] * fix, axis=1, keepdims=True)
    out[:, 2:3, :] = jnp.sum(weighted[...] * fix, axis=1, keepdims=True)


def grad_kernel(where, seg_blocks, seg_audio, *refs):
    q_refs, o_refs, st_refs = refs[:NY], refs[NY : 2 * NY], refs[2 * NY : 3 * NY]
    (z_ref, c_ref, dq_out, own_out, other_out, q_buf, o_buf, kv_buf, lse, delta, dq, dk, dv, sem) = (
        refs[3 * NY :]
    )
    load_all(where, q_refs, o_refs, z_ref, c_ref, q_buf, o_buf, kv_buf, sem)
    ends = span_ends(where, seg_blocks, seg_audio)
    tops = [ref[:, 0:1, :] for ref in st_refs]
    top = jnp.maximum(jnp.maximum(tops[0], tops[1]), jnp.maximum(tops[2], tops[3]))
    fixes = [jnp.exp2(t - top) for t in tops]
    total = sum(f * ref[:, 1:2, :] for f, ref in zip(fixes, st_refs))
    lse[...] = top + jnp.log2(total)
    delta[...] = sum(f * ref[:, 2:3, :] for f, ref in zip(fixes, st_refs)) / total
    dq[...] = jnp.zeros_like(dq)
    dk[...] = jnp.zeros_like(dk)
    dv[...] = jnp.zeros_like(dv)

    def pair(j, i, count, masked):
        k = kv_buf[0, j].reshape(COL, DH)[:count]
        v = kv_buf[1, j].reshape(COL, DH)[:count]
        p_parts, ds_parts = [], []
        for r in range(0, ROWS, RB):
            rows = slice(r, r + RB)
            s = dot_nt(k, q_buf[i, rows, :]) * SCALE2
            p = jnp.exp2(s - lse[i, :, rows])
            if masked:
                p = jnp.where(visible(where, ends, j, i, count, r, RB), p, 0.0)
            dp = dot_nt(v, o_buf[i, rows, :])
            ds = (p * (dp - delta[i, :, rows])).astype(BF)
            dq[i, :, rows] += dot_tn(k, ds)
            p_parts.append(p.astype(BF))
            ds_parts.append(ds)
        dv[j, :count, :] += dot_nn(jnp.concatenate(p_parts, axis=1), o_buf[i])
        dk[j, :count, :] += dot_nn(jnp.concatenate(ds_parts, axis=1), q_buf[i])

    each_pair(ends, pair)
    y, z, c, x = (where[n] for n in range(4))
    for d in range(NY):
        dq_out[d] = (dq[lax.rem(y + d, NY)].T * SCALE).astype(BF)
    for d in range(NZ):
        first = lax.rem(z + d, NZ) * NC
        for r in range(NX):
            j = lax.rem(x + NX - r, NX)
            for block, out in ((first + c, own_out), (first + 1 - c, other_out)):
                rows = pl.ds(pl.multiple_of(block * SLICE, SLICE), SLICE)
                out[d, r, 0] = dk[j, rows, :] * SCALE
                out[d, r, 1] = dv[j, rows, :]


def buffers():
    return [
        pltpu.VMEM((NY, ROWS, DH), BF),
        pltpu.VMEM((NY, ROWS, DH), BF),
        pltpu.VMEM((2, NY, NZ * NC, SLICE, DH), BF),
    ]


def stats_call(where, seg_blocks, seg_audio, q, o, z_all, c_all):
    return pl.pallas_call(
        stats_kernel,
        out_shape=jax.ShapeDtypeStruct((NY, 3, ROWS), F32),
        in_specs=[SM] * 3 + [HB] * (2 * NY + 2),
        out_specs=VM,
        scratch_shapes=buffers()
        + [pltpu.VMEM((NY, 8, ROWS), F32)] * 3
        + [pltpu.SemaphoreType.DMA((1,))],
        compiler_params=pltpu.CompilerParams(vmem_limit_bytes=56 << 20),
        name="stats",
    )(where, seg_blocks, seg_audio, *q, *o, z_all, c_all)


def grad_call(where, seg_blocks, seg_audio, q, o, st, z_all, c_all):
    part = jax.ShapeDtypeStruct((NZ, NX, 2, SLICE, DH), F32)
    return pl.pallas_call(
        grad_kernel,
        out_shape=(jax.ShapeDtypeStruct((NY, ROWS, DH), BF), part, part),
        in_specs=[SM] * 3 + [HB] * (2 * NY) + [VM] * NY + [HB] * 2,
        out_specs=(VM,) * 3,
        scratch_shapes=buffers()
        + [
            pltpu.VMEM((NY, 1, ROWS), F32),
            pltpu.VMEM((NY, 1, ROWS), F32),
            pltpu.VMEM((NY, DH, ROWS), F32),
            pltpu.VMEM((NY, COL, DH), F32),
            pltpu.VMEM((NY, COL, DH), F32),
            pltpu.SemaphoreType.DMA((1,)),
        ],
        compiler_params=pltpu.CompilerParams(vmem_limit_bytes=56 << 20),
        name="grads",
    )(where, seg_blocks, seg_audio, *q, *o, *st, z_all, c_all)


def shift(value, axis, size, by):
    return lax.ppermute(value, axis, [((n + by) % size, n) for n in range(size)])


def body(query, key, value, d_out, seg_blocks, seg_audio):
    y, z, c, x = (lax.axis_index(name).astype(jnp.int32) for name in ("y", "z", "c", "x"))
    where = jnp.stack([y, z, c, x])
    heads = jnp.stack([key, value]).transpose(2, 0, 1, 3)
    rounds = []
    for r in range(NX):
        piece = lax.dynamic_index_in_dim(heads, (y + r) % NX, 0, keepdims=False)
        perm = [
            (b * NX + a, a * NX + (b + r) % NX) for b in range(NY) for a in range(NX)
        ]
        rounds.append(lax.ppermute(piece, ("y", "x"), perm))
    own = jnp.stack(rounds)
    q0, o0 = query.reshape(ROWS, DH), d_out.reshape(ROWS, DH)
    q1, q3 = shift(q0, "y", NY, 1), shift(q0, "y", NY, -1)
    o1, o3 = shift(o0, "y", NY, 1), shift(o0, "y", NY, -1)
    q2, o2 = shift(q1, "y", NY, 1), shift(o3, "y", NY, -1)
    z_all = jnp.stack([own] + [shift(own, "z", NZ, -d) for d in range(1, NZ)])
    c_all = shift(z_all, "c", NC, 1)
    q, o = (q0, q1, q2, q3), (o0, o1, o2, o3)
    st = stats_call(where, seg_blocks, seg_audio, q, o, z_all, c_all)
    sts = (st,) + tuple(shift(st, "y", NY, d) for d in range(1, NY))
    dq, own_part, other_part = grad_call(
        where, seg_blocks, seg_audio, q, o, sts, z_all, c_all
    )
    dq_sum = dq[0].astype(F32)
    for d in range(1, NY):
        dq_sum = dq_sum + shift(dq[d], "y", NY, -d).astype(F32)
    d_query = dq_sum.astype(BF).reshape(BLK, GROUP, DH)
    both = own_part + shift(other_part, "c", NC, 1)
    low = both.astype(BF)
    kv_sum = both[0]
    for d in range(1, NZ):
        kv_sum = kv_sum + shift(low[d], "z", NZ, -d).astype(F32)
    kv_low = kv_sum.astype(BF)
    back = []
    for r in range(NX):
        perm = [
            (a * NX + (b + r) % NX, b * NX + a) for b in range(NY) for a in range(NX)
        ]
        back.append(lax.ppermute(kv_low[r], ("y", "x"), perm))
    ring = jnp.stack(back + back)
    ring = lax.dynamic_slice_in_dim(ring, (NX - y) % NX, NX, axis=0)
    ring = ring.transpose(1, 2, 0, 3)
    return (d_query, ring[0], ring[1])


def solution(mesh):
    fine = Mesh(mesh.devices.reshape(NY, NZ, NC, NX), ("y", "z", "c", "x"))
    ctx = ("y", "z", "c")
    rows, tokens = P(ctx, "x", None), P(("y", "z", "c", "x"), None, None)
    return jax.shard_map(
        body,
        mesh=fine,
        in_specs=(rows, tokens, tokens, rows, P(), P()),
        out_specs=(rows, tokens, tokens),
        check_vma=False,
    )
```

```python
import math

import jax
import jax.numpy as jnp
from jax import lax
from jax.experimental import pallas as pl
from jax.experimental.pallas import tpu as pltpu
from jax.sharding import Mesh, PartitionSpec as P


DH = 128
GROUP = 8
BLK = 128
NY, NZ, NC, NX = 4, 8, 2, 4
NSEG = 32
ROWS = BLK * GROUP
SLICE = BLK // NY
COL = NZ * NC * SLICE
NEG = -1e30
SCALE = 1.0 / math.sqrt(DH)
SCALE2 = SCALE * math.log2(math.e)
RB = 1024
CROSS = 4 * SLICE
BF, F32 = jnp.bfloat16, jnp.float32
VM = pl.BlockSpec(memory_space=pltpu.VMEM)
SM = pl.BlockSpec(memory_space=pltpu.SMEM)
HB = pl.BlockSpec(memory_space=pl.ANY)


def dot_nt(a, b):
    return lax.dot_general(a, b, (((1,), (1,)), ((), ())), preferred_element_type=F32)


def dot_nn(a, b):
    return lax.dot_general(a, b, (((1,), (0,)), ((), ())), preferred_element_type=F32)


def dot_tn(a, b):
    return lax.dot_general(a, b, (((0,), (0,)), ((), ())), preferred_element_type=F32)


def span_ends(where, seg_blocks, seg_audio):
    blocks = [i * NZ * NC + where[1] * NC + where[2] for i in range(NY)]

    def step(s, carry):
        start, found = carry
        end = start + seg_blocks[s]
        value = jnp.where(seg_audio[s] == 1, end * BLK, 0)
        found = tuple(
            jnp.where((start <= b) & (b < end), value, f) for b, f in zip(blocks, found)
        )
        return (end, found)

    zero = jnp.int32(0)
    return lax.fori_loop(0, NSEG, step, (zero, (zero,) * NY))[1]


def pick(i, values):
    out = values[0]
    for n in range(1, len(values)):
        out = jnp.where(i == n, values[n], out)
    return out


def place():
    return tuple(lax.axis_index(name).astype(jnp.int32) for name in ("y", "z", "c", "x"))


def load_all(where, q_refs, o_refs, z_ref, c_ref, q_buf, o_buf, kv_buf, sem):
    y, _, c, x = where
    for r in range(NX):
        j = lax.rem(x + NX - r, NX)
        for e, ref in enumerate((z_ref, c_ref)):
            for d in range(NZ):
                block = d * NC + (c if e == 0 else 1 - c)
                pltpu.make_async_copy(
                    ref.at[d, r], kv_buf.at[:, j, block], sem.at[NY + j]
                ).start()
    for d in range(NY):
        i = lax.rem(y + d, NY)
        pltpu.make_async_copy(q_refs[d], q_buf.at[i], sem.at[i]).start()
        pltpu.make_async_copy(o_refs[d], o_buf.at[i], sem.at[i]).start()


def wait_for(i, q_buf, o_buf, kv_buf, sem):
    pltpu.make_async_copy(q_buf.at[i], q_buf.at[i], sem.at[i]).wait()
    pltpu.make_async_copy(o_buf.at[i], o_buf.at[i], sem.at[i]).wait()
    pltpu.make_async_copy(kv_buf.at[:, i], kv_buf.at[:, i], sem.at[NY + i]).wait()


def visible(where, ends, j, i, count, rows_from, rows):
    n = lax.broadcasted_iota(jnp.int32, (count, 1), 0)
    key_pos = (j * NZ * NC + n // SLICE) * BLK + where[0] * SLICE + n % SLICE
    r = lax.broadcasted_iota(jnp.int32, (1, rows), 1) + rows_from
    query_pos = (i * NZ * NC + where[1] * NC + where[2]) * BLK + r // GROUP
    return key_pos < jnp.maximum(query_pos + 1, pick(i, ends))


def each_pair(ends, pair, ready):
    def full(p, carry):
        i = 1 + (p >= 1).astype(jnp.int32) + (p >= 3).astype(jnp.int32)
        pair(p - i * (i - 1) // 2, i, COL, False, False)
        return carry

    def diagonal(i, carry):
        ready(i)
        pair(i, i, COL, True, True)
        return carry

    def crossing(i, carry):
        @pl.when(pick(i, ends) > (i + 1) * NZ * NC * BLK)
        def _():
            pair(i + 1, i, CROSS, True, False)

        return carry

    lax.fori_loop(0, NY, diagonal, 0)
    lax.fori_loop(0, NY * (NY - 1) // 2, full, 0)
    lax.fori_loop(0, NY - 1, crossing, 0)


def stats_kernel(seg_blocks, seg_audio, *refs):
    q_refs, o_refs = refs[:NY], refs[NY : 2 * NY]
    z_ref, c_ref, out, q_buf, o_buf, kv_buf, high, total, weighted, sem = refs[2 * NY :]
    where = place()
    load_all(where, q_refs, o_refs, z_ref, c_ref, q_buf, o_buf, kv_buf, sem)
    ends = span_ends(where, seg_blocks, seg_audio)
    high[...] = jnp.full_like(high, NEG)
    total[...] = jnp.zeros_like(total)
    weighted[...] = jnp.zeros_like(weighted)

    def pair(j, i, count, masked, first):
        k = kv_buf[0, j].reshape(COL, DH)[:count]
        v = kv_buf[1, j].reshape(COL, DH)[:count]
        for r in range(0, ROWS, RB):
            rows = slice(r, r + RB)
            s = dot_nt(k, q_buf[i, rows, :]) * SCALE2
            if masked:
                seen = visible(where, ends, j, i, count, r, RB)
                s = jnp.where(seen, s, NEG)
            dp = dot_nt(v, o_buf[i, rows, :]).reshape(count // 8, 8, RB)
            s = s.reshape(count // 8, 8, RB)
            old = high[i, :, rows]
            new = jnp.maximum(old, jnp.max(s, axis=0))
            fix = jnp.exp2(old - new)
            p = jnp.exp2(s - new[None])
            if masked:
                p = jnp.where(seen.reshape(count // 8, 8, RB), p, 0.0)
            high[i, :, rows] = new
            total[i, :, rows] = total[i, :, rows] * fix + jnp.sum(p, axis=0)
            weighted[i, :, rows] = weighted[i, :, rows] * fix + jnp.sum(p * dp, axis=0)

    each_pair(ends, pair, lambda i: wait_for(i, q_buf, o_buf, kv_buf, sem))
    top = jnp.max(high[...], axis=1, keepdims=True)
    fix = jnp.exp2(high[...] - top)
    out[:, 0:1, :] = top
    out[:, 1:2, :] = jnp.sum(total[...] * fix, axis=1, keepdims=True)
    out[:, 2:3, :] = jnp.sum(weighted[...] * fix, axis=1, keepdims=True)


def grad_kernel(seg_blocks, seg_audio, *refs):
    q_refs, o_refs, st_refs = refs[:NY], refs[NY : 2 * NY], refs[2 * NY : 3 * NY]
    z_ref, c_ref = refs[3 * NY : 3 * NY + 2]
    dq_outs, (own_out, other_out) = refs[3 * NY + 2 : 4 * NY + 2], refs[4 * NY + 2 : 4 * NY + 4]
    q_buf, o_buf, kv_buf, st_buf, lse, delta, dq, dk, dv, sem, st_sem = refs[4 * NY + 4 :]
    for d in range(NY):
        pltpu.make_async_copy(st_refs[d], st_buf.at[d], st_sem.at[0]).start()
    where = place()
    load_all(where, q_refs, o_refs, z_ref, c_ref, q_buf, o_buf, kv_buf, sem)
    ends = span_ends(where, seg_blocks, seg_audio)
    pltpu.make_async_copy(st_buf, st_buf, st_sem.at[0]).wait()
    top = jnp.max(st_buf[:, :, 0:1, :], axis=0)
    fix = jnp.exp2(st_buf[:, :, 0:1, :] - top[None])
    total = jnp.sum(fix * st_buf[:, :, 1:2, :], axis=0)
    lse[...] = top + jnp.log2(total)
    delta[...] = jnp.sum(fix * st_buf[:, :, 2:3, :], axis=0) / total

    def pair(j, i, count, masked, first):
        k = kv_buf[0, j].reshape(COL, DH)[:count]
        v = kv_buf[1, j].reshape(COL, DH)[:count]
        p_parts, ds_parts = [], []
        for r in range(0, ROWS, RB):
            rows = slice(r, r + RB)
            s = dot_nt(k, q_buf[i, rows, :]) * SCALE2
            p = jnp.exp2(s - lse[i, :, rows])
            if masked:
                p = jnp.where(visible(where, ends, j, i, count, r, RB), p, 0.0)
            dp = dot_nt(v, o_buf[i, rows, :])
            ds = (p * (dp - delta[i, :, rows])).astype(BF)
            if first:
                dq[i, :, rows] = dot_tn(k, ds)
            else:
                dq[i, :, rows] += dot_tn(k, ds)
            p_parts.append(p.astype(BF))
            ds_parts.append(ds)
        dv_part = dot_nn(jnp.concatenate(p_parts, axis=1), o_buf[i])
        dk_part = dot_nn(jnp.concatenate(ds_parts, axis=1), q_buf[i])
        if first:
            dv[j, :count, :] = dv_part
            dk[j, :count, :] = dk_part
        else:
            dv[j, :count, :] += dv_part
            dk[j, :count, :] += dk_part

    each_pair(ends, pair, lambda i: wait_for(i, q_buf, o_buf, kv_buf, sem))
    y, z, c, x = where
    for d in range(NY):
        dq_outs[d][...] = (dq[lax.rem(y + d, NY)].T * SCALE).astype(BF)
    for d in range(NZ):
        first = lax.rem(z + d, NZ) * NC
        for r in range(NX):
            j = lax.rem(x + NX - r, NX)
            for block, out in ((first + c, own_out), (first + 1 - c, other_out)):
                rows = pl.ds(pl.multiple_of(block * SLICE, SLICE), SLICE)
                out[d, r, 0] = dk[j, rows, :] * SCALE
                out[d, r, 1] = dv[j, rows, :]


def buffers():
    return [
        pltpu.VMEM((NY, ROWS, DH), BF),
        pltpu.VMEM((NY, ROWS, DH), BF),
        pltpu.VMEM((2, NY, NZ * NC, SLICE, DH), BF),
    ]


def stats_call(seg_blocks, seg_audio, q, o, z_all, c_all):
    return pl.pallas_call(
        stats_kernel,
        out_shape=jax.ShapeDtypeStruct((NY, 3, ROWS), F32),
        in_specs=[SM] * 2 + [HB] * (2 * NY + 2),
        out_specs=VM,
        scratch_shapes=buffers()
        + [pltpu.VMEM((NY, 8, ROWS), F32)] * 3
        + [pltpu.SemaphoreType.DMA((2 * NY,))],
        compiler_params=pltpu.CompilerParams(vmem_limit_bytes=56 << 20),
        name="stats",
    )(seg_blocks, seg_audio, *q, *o, z_all, c_all)


def grad_call(seg_blocks, seg_audio, q, o, st, z_all, c_all):
    part = jax.ShapeDtypeStruct((NZ, NX, 2, SLICE, DH), F32)
    return pl.pallas_call(
        grad_kernel,
        out_shape=(jax.ShapeDtypeStruct((ROWS, DH), BF),) * NY + (part, part),
        in_specs=[SM] * 2 + [HB] * (3 * NY + 2),
        out_specs=(VM,) * (NY + 2),
        scratch_shapes=buffers()
        + [
            pltpu.VMEM((NY, NY, 3, ROWS), F32),
            pltpu.VMEM((NY, 1, ROWS), F32),
            pltpu.VMEM((NY, 1, ROWS), F32),
            pltpu.VMEM((NY, DH, ROWS), F32),
            pltpu.VMEM((NY, COL, DH), F32),
            pltpu.VMEM((NY, COL, DH), F32),
            pltpu.SemaphoreType.DMA((2 * NY,)),
            pltpu.SemaphoreType.DMA((1,)),
        ],
        compiler_params=pltpu.CompilerParams(vmem_limit_bytes=56 << 20),
        name="grads",
    )(seg_blocks, seg_audio, *q, *o, *st, z_all, c_all)


def shift(value, axis, size, by):
    return lax.ppermute(value, axis, [((n + by) % size, n) for n in range(size)])


def steps(query, key, value, d_out, seg_blocks, seg_audio):
    y, _, _, _ = (lax.axis_index(name).astype(jnp.int32) for name in ("y", "z", "c", "x"))
    heads = jnp.stack([key, value]).transpose(2, 0, 1, 3)
    rounds = []
    for r in range(NX):
        piece = lax.dynamic_index_in_dim(heads, (y + r) % NX, 0, keepdims=False)
        perm = [
            (b * NX + a, a * NX + (b + r) % NX) for b in range(NY) for a in range(NX)
        ]
        rounds.append(lax.ppermute(piece, ("y", "x"), perm))
    own = jnp.stack(rounds)
    q0, o0 = query.reshape(ROWS, DH), d_out.reshape(ROWS, DH)
    q1, q3 = shift(q0, "y", NY, 1), shift(q0, "y", NY, -1)
    o1, o3 = shift(o0, "y", NY, 1), shift(o0, "y", NY, -1)
    q2, o2 = shift(q1, "y", NY, 1), shift(o3, "y", NY, -1)
    z_all = lax.all_to_all(jnp.broadcast_to(own[None], (NZ,) + own.shape), "z", 0, 0)
    c_all = shift(z_all, "c", NC, 1)
    q, o = (q0, q1, q2, q3), (o0, o1, o2, o3)
    st = stats_call(seg_blocks, seg_audio, q, o, z_all, c_all)
    sts = (st,) + tuple(shift(st, "y", NY, d) for d in range(1, NY))
    *dq, own_part, other_part = grad_call(
        seg_blocks, seg_audio, q, o, sts, z_all, c_all
    )
    dq_sum = dq[0].astype(F32)
    for d in range(1, NY):
        dq_sum = dq_sum + shift(dq[d], "y", NY, -d).astype(F32)
    d_query = dq_sum.astype(BF).reshape(BLK, GROUP, DH)
    both = own_part + shift(other_part, "c", NC, 1)
    low = both.astype(BF)
    kv_sum = both[0]
    for d in range(1, NZ):
        kv_sum = kv_sum + shift(low[d], "z", NZ, -d).astype(F32)
    kv_low = kv_sum.astype(BF)
    back = []
    for r in range(NX):
        perm = [
            (a * NX + (b + r) % NX, b * NX + a) for b in range(NY) for a in range(NX)
        ]
        back.append(lax.ppermute(kv_low[r], ("y", "x"), perm))
    ring = jnp.stack(back + back)
    ring = lax.dynamic_slice_in_dim(ring, (NX - y) % NX, NX, axis=0)
    ring = ring.transpose(1, 2, 0, 3)
    return (d_query, ring[0], ring[1])


def solution(mesh):
    fine = Mesh(mesh.devices.reshape(NY, NZ, NC, NX), ("y", "z", "c", "x"))
    ctx = ("y", "z", "c")
    rows, tokens = P(ctx, "x", None), P(("y", "z", "c", "x"), None, None)
    return jax.shard_map(
        steps,
        mesh=fine,
        in_specs=(rows, tokens, tokens, rows, P(), P()),
        out_specs=(rows, tokens, tokens),
        check_vma=False,
    )
```

```python
import math

import jax
import jax.numpy as jnp
from jax import lax
from jax.experimental import pallas as pl
from jax.experimental.pallas import tpu as pltpu
from jax.sharding import Mesh, PartitionSpec as P


DH = 128
GROUP = 8
BLK = 128
NY, NZ, NC, NX = 4, 8, 2, 4
NSEG = 32
ROWS = BLK * GROUP
SLICE = BLK // NY
COL = NZ * NC * SLICE
NEG = -1e30
SCALE = 1.0 / math.sqrt(DH)
SCALE2 = SCALE * math.log2(math.e)
RB = 1024
CROSS = 4 * SLICE
BF, F32 = jnp.bfloat16, jnp.float32
VM = pl.BlockSpec(memory_space=pltpu.VMEM)
SM = pl.BlockSpec(memory_space=pltpu.SMEM)
HB = pl.BlockSpec(memory_space=pl.ANY)


def dot_nt(a, b):
    return lax.dot_general(a, b, (((1,), (1,)), ((), ())), preferred_element_type=F32)


def dot_nn(a, b):
    return lax.dot_general(a, b, (((1,), (0,)), ((), ())), preferred_element_type=F32)


def dot_tn(a, b):
    return lax.dot_general(a, b, (((0,), (0,)), ((), ())), preferred_element_type=F32)


def span_ends(where, seg_blocks, seg_audio):
    blocks = [i * NZ * NC + where[1] * NC + where[2] for i in range(NY)]

    def step(s, carry):
        start, found = carry
        end = start + seg_blocks[s]
        value = jnp.where(seg_audio[s] == 1, end * BLK, 0)
        found = tuple(
            jnp.where((start <= b) & (b < end), value, f) for b, f in zip(blocks, found)
        )
        return (end, found)

    zero = jnp.int32(0)
    return lax.fori_loop(0, NSEG, step, (zero, (zero,) * NY))[1]


def pick(i, values):
    out = values[0]
    for n in range(1, len(values)):
        out = jnp.where(i == n, values[n], out)
    return out


def place():
    return tuple(lax.axis_index(name).astype(jnp.int32) for name in ("y", "z", "c", "x"))


def load_all(where, q_refs, o_refs, z_ref, c_ref, q_buf, o_buf, kv_buf, sem):
    y, _, c, x = where
    for r in range(NX):
        j = lax.rem(x + NX - r, NX)
        for e, ref in enumerate((z_ref, c_ref)):
            for d in range(NZ):
                block = d * NC + (c if e == 0 else 1 - c)
                pltpu.make_async_copy(
                    ref.at[d, r], kv_buf.at[:, j, block], sem.at[NY + j]
                ).start()
    for d in range(NY):
        i = lax.rem(y + d, NY)
        pltpu.make_async_copy(q_refs[d], q_buf.at[i], sem.at[i]).start()
        pltpu.make_async_copy(o_refs[d], o_buf.at[i], sem.at[i]).start()


def wait_for(i, q_buf, o_buf, kv_buf, sem):
    pltpu.make_async_copy(q_buf.at[i], q_buf.at[i], sem.at[i]).wait()
    pltpu.make_async_copy(o_buf.at[i], o_buf.at[i], sem.at[i]).wait()
    pltpu.make_async_copy(kv_buf.at[:, i], kv_buf.at[:, i], sem.at[NY + i]).wait()


def visible(where, ends, j, i, count, rows_from, rows):
    n = lax.broadcasted_iota(jnp.int32, (count, 1), 0)
    key_pos = (j * NZ * NC + n // SLICE) * BLK + where[0] * SLICE + n % SLICE
    r = lax.broadcasted_iota(jnp.int32, (1, rows), 1) + rows_from
    query_pos = (i * NZ * NC + where[1] * NC + where[2]) * BLK + r // GROUP
    return key_pos < jnp.maximum(query_pos + 1, pick(i, ends))


def each_pair(ends, pair, ready):
    def full(p, carry):
        i = 1 + (p >= 1).astype(jnp.int32) + (p >= 3).astype(jnp.int32)
        pair(p - i * (i - 1) // 2, i, COL, False, False)
        return carry

    def diagonal(i, carry):
        ready(i)
        pair(i, i, COL, True, True)
        return carry

    def crossing(i, carry):
        @pl.when(pick(i, ends) > (i + 1) * NZ * NC * BLK)
        def _():
            pair(i + 1, i, CROSS, True, False)

        return carry

    lax.fori_loop(0, NY, diagonal, 0)
    lax.fori_loop(0, NY * (NY - 1) // 2, full, 0)
    lax.fori_loop(0, NY - 1, crossing, 0)


def stats_kernel(seg_blocks, seg_audio, *refs):
    q_refs, o_refs = refs[:NY], refs[NY : 2 * NY]
    z_ref, c_ref, out, q_buf, o_buf, kv_buf, high, total, weighted, sem = refs[2 * NY :]
    where = place()
    load_all(where, q_refs, o_refs, z_ref, c_ref, q_buf, o_buf, kv_buf, sem)
    ends = span_ends(where, seg_blocks, seg_audio)
    high[...] = jnp.full_like(high, NEG)
    total[...] = jnp.zeros_like(total)
    weighted[...] = jnp.zeros_like(weighted)

    def pair(j, i, count, masked, first):
        k = kv_buf[0, j].reshape(COL, DH)[:count]
        v = kv_buf[1, j].reshape(COL, DH)[:count]
        for r in range(0, ROWS, RB):
            rows = slice(r, r + RB)
            s = dot_nt(k, q_buf[i, rows, :]) * SCALE2
            if masked:
                seen = visible(where, ends, j, i, count, r, RB)
                s = jnp.where(seen, s, NEG)
            dp = dot_nt(v, o_buf[i, rows, :]).reshape(count // 8, 8, RB)
            s = s.reshape(count // 8, 8, RB)
            old = high[i, :, rows]
            new = jnp.maximum(old, jnp.max(s, axis=0))
            fix = jnp.exp2(old - new)
            p = jnp.exp2(s - new[None])
            if masked:
                p = jnp.where(seen.reshape(count // 8, 8, RB), p, 0.0)
            high[i, :, rows] = new
            total[i, :, rows] = total[i, :, rows] * fix + jnp.sum(p, axis=0)
            weighted[i, :, rows] = weighted[i, :, rows] * fix + jnp.sum(p * dp, axis=0)

    each_pair(ends, pair, lambda i: wait_for(i, q_buf, o_buf, kv_buf, sem))
    top = jnp.max(high[...], axis=1, keepdims=True)
    fix = jnp.exp2(high[...] - top)
    out[:, 0:1, :] = top
    out[:, 1:2, :] = jnp.sum(total[...] * fix, axis=1, keepdims=True)
    out[:, 2:3, :] = jnp.sum(weighted[...] * fix, axis=1, keepdims=True)


def grad_kernel(seg_blocks, seg_audio, *refs):
    q_refs, o_refs, st_refs = refs[:NY], refs[NY : 2 * NY], refs[2 * NY : 3 * NY]
    z_ref, c_ref = refs[3 * NY : 3 * NY + 2]
    dq_outs, (own_out, other_out) = refs[3 * NY + 2 : 4 * NY + 2], refs[4 * NY + 2 : 4 * NY + 4]
    q_buf, o_buf, kv_buf, st_buf, lse, delta, dq, dk, dv, sem, st_sem = refs[4 * NY + 4 :]
    for d in range(NY):
        pltpu.make_async_copy(st_refs[d], st_buf.at[d], st_sem.at[0]).start()
    where = place()
    load_all(where, q_refs, o_refs, z_ref, c_ref, q_buf, o_buf, kv_buf, sem)
    ends = span_ends(where, seg_blocks, seg_audio)
    pltpu.make_async_copy(st_buf, st_buf, st_sem.at[0]).wait()
    top = jnp.max(st_buf[:, :, 0:1, :], axis=0)
    fix = jnp.exp2(st_buf[:, :, 0:1, :] - top[None])
    total = jnp.sum(fix * st_buf[:, :, 1:2, :], axis=0)
    lse[...] = top + jnp.log2(total)
    delta[...] = jnp.sum(fix * st_buf[:, :, 2:3, :], axis=0) / total

    def pair(j, i, count, masked, first):
        k = kv_buf[0, j].reshape(COL, DH)[:count]
        v = kv_buf[1, j].reshape(COL, DH)[:count]
        p_parts, ds_parts = [], []
        for r in range(0, ROWS, RB):
            rows = slice(r, r + RB)
            s = dot_nt(k, q_buf[i, rows, :]) * SCALE2
            p = jnp.exp2(s - lse[i, :, rows])
            if masked:
                p = jnp.where(visible(where, ends, j, i, count, r, RB), p, 0.0)
            dp = dot_nt(v, o_buf[i, rows, :])
            ds = (p * (dp - delta[i, :, rows])).astype(BF)
            if first:
                dq[i, :, rows] = dot_tn(k, ds)
            else:
                dq[i, :, rows] += dot_tn(k, ds)
            p_parts.append(p.astype(BF))
            ds_parts.append(ds)
        dv_part = dot_nn(jnp.concatenate(p_parts, axis=1), o_buf[i])
        dk_part = dot_nn(jnp.concatenate(ds_parts, axis=1), q_buf[i])
        if first:
            dv[j, :count, :] = dv_part
            dk[j, :count, :] = dk_part
        else:
            dv[j, :count, :] += dv_part
            dk[j, :count, :] += dk_part

    each_pair(ends, pair, lambda i: wait_for(i, q_buf, o_buf, kv_buf, sem))
    y, z, c, x = where
    for d in range(NY):
        dq_outs[d][...] = (dq[lax.rem(y + d, NY)].T * SCALE).astype(BF)
    for d in range(NZ):
        first = lax.rem(z + d, NZ) * NC
        for r in range(NX):
            j = lax.rem(x + NX - r, NX)
            for block, out in ((first + c, own_out), (first + 1 - c, other_out)):
                rows = pl.ds(pl.multiple_of(block * SLICE, SLICE), SLICE)
                out[d, r, 0] = dk[j, rows, :] * SCALE
                out[d, r, 1] = dv[j, rows, :]


def buffers():
    return [
        pltpu.VMEM((NY, ROWS, DH), BF),
        pltpu.VMEM((NY, ROWS, DH), BF),
        pltpu.VMEM((2, NY, NZ * NC, SLICE, DH), BF),
    ]


def near(value):
    return pltpu.with_memory_space_constraint(value, pltpu.VMEM)


def stats_call(seg_blocks, seg_audio, q, o, z_all, c_all):
    return pl.pallas_call(
        stats_kernel,
        out_shape=pltpu.VMEM((NY, 3, ROWS), F32),
        in_specs=[SM] * 2 + [HB] * (2 * NY + 2),
        out_specs=VM,
        scratch_shapes=buffers()
        + [pltpu.VMEM((NY, 8, ROWS), F32)] * 3
        + [pltpu.SemaphoreType.DMA((2 * NY,))],
        compiler_params=pltpu.CompilerParams(vmem_limit_bytes=24 << 20),
        name="stats",
    )(seg_blocks, seg_audio, *map(near, (*q, *o, z_all, c_all)))


def grad_call(seg_blocks, seg_audio, q, o, st, z_all, c_all):
    part = pltpu.VMEM((NZ, NX, 2, SLICE, DH), F32)
    return pl.pallas_call(
        grad_kernel,
        out_shape=(pltpu.VMEM((ROWS, DH), BF),) * NY + (part, part),
        in_specs=[SM] * 2 + [HB] * (3 * NY + 2),
        out_specs=(VM,) * (NY + 2),
        scratch_shapes=buffers()
        + [
            pltpu.VMEM((NY, NY, 3, ROWS), F32),
            pltpu.VMEM((NY, 1, ROWS), F32),
            pltpu.VMEM((NY, 1, ROWS), F32),
            pltpu.VMEM((NY, DH, ROWS), F32),
            pltpu.VMEM((NY, COL, DH), F32),
            pltpu.VMEM((NY, COL, DH), F32),
            pltpu.SemaphoreType.DMA((2 * NY,)),
            pltpu.SemaphoreType.DMA((1,)),
        ],
        compiler_params=pltpu.CompilerParams(vmem_limit_bytes=24 << 20),
        name="grads",
    )(seg_blocks, seg_audio, *map(near, (*q, *o, *st, z_all, c_all)))


def shift(value, axis, size, by):
    return lax.ppermute(value, axis, [((n + by) % size, n) for n in range(size)])


def steps(query, key, value, d_out, seg_blocks, seg_audio):
    y, _, _, _ = (lax.axis_index(name).astype(jnp.int32) for name in ("y", "z", "c", "x"))
    heads = jnp.stack([key, value]).transpose(2, 0, 1, 3)
    rounds = []
    for r in range(NX):
        piece = lax.dynamic_index_in_dim(heads, (y + r) % NX, 0, keepdims=False)
        perm = [
            (b * NX + a, a * NX + (b + r) % NX) for b in range(NY) for a in range(NX)
        ]
        rounds.append(lax.ppermute(piece, ("y", "x"), perm))
    own = jnp.stack(rounds)
    q0, o0 = query.reshape(ROWS, DH), d_out.reshape(ROWS, DH)
    q1, q3 = shift(q0, "y", NY, 1), shift(q0, "y", NY, -1)
    o1, o3 = shift(o0, "y", NY, 1), shift(o0, "y", NY, -1)
    q2, o2 = shift(q1, "y", NY, 1), shift(o3, "y", NY, -1)
    z_all = lax.all_to_all(jnp.broadcast_to(own[None], (NZ,) + own.shape), "z", 0, 0)
    c_all = shift(z_all, "c", NC, 1)
    q, o = (q0, q1, q2, q3), (o0, o1, o2, o3)
    st = stats_call(seg_blocks, seg_audio, q, o, z_all, c_all)
    sts = (st,) + tuple(shift(st, "y", NY, d) for d in range(1, NY))
    *dq, own_part, other_part = grad_call(
        seg_blocks, seg_audio, q, o, sts, z_all, c_all
    )
    dq_parts = [shift(dq[d], "y", NY, -d) for d in range(1, NY)]
    dq_sum = dq[0].astype(F32)
    for part in dq_parts:
        dq_sum = dq_sum + part.astype(F32)
    d_query = dq_sum.astype(BF).reshape(BLK, GROUP, DH)
    both = own_part + shift(other_part, "c", NC, 1)
    low = both.astype(BF)
    carried = shift(low[4], "z", NZ, -1)
    third = (both[3] + carried.astype(F32)).astype(BF)
    kv_sum = both[0] + shift(third, "z", NZ, -3).astype(F32)
    for d in (1, 2, 5, 6, 7):
        kv_sum = kv_sum + shift(low[d], "z", NZ, -d).astype(F32)
    kv_low = kv_sum.astype(BF)
    back = []
    for r in range(NX):
        perm = [
            (a * NX + (b + r) % NX, b * NX + a) for b in range(NY) for a in range(NX)
        ]
        back.append(lax.ppermute(kv_low[r], ("y", "x"), perm))
    ring = jnp.stack(back + back)
    ring = lax.dynamic_slice_in_dim(ring, (NX - y) % NX, NX, axis=0)
    ring = ring.transpose(1, 2, 0, 3)
    return (d_query, ring[0], ring[1])


def solution(mesh):
    fine = Mesh(mesh.devices.reshape(NY, NZ, NC, NX), ("y", "z", "c", "x"))
    ctx = ("y", "z", "c")
    rows, tokens = P(ctx, "x", None), P(("y", "z", "c", "x"), None, None)
    return jax.shard_map(
        steps,
        mesh=fine,
        in_specs=(rows, tokens, tokens, rows, P(), P()),
        out_specs=(rows, tokens, tokens),
        check_vma=False,
    )
```

```python
import math

import jax
import jax.numpy as jnp
from jax import lax
from jax.experimental import pallas as pl
from jax.experimental.pallas import tpu as pltpu
from jax.sharding import Mesh, PartitionSpec as P


DH = 128
GROUP = 8
BLK = 128
NY, NZ, NC, NX = 4, 8, 2, 4
NSEG = 32
ROWS = BLK * GROUP
SLICE = BLK // NY
COL = NZ * NC * SLICE
NEG = -1e30
SCALE = 1.0 / math.sqrt(DH)
SCALE2 = SCALE * math.log2(math.e)
RB = 1024
CROSS = 4 * SLICE
BF, F32 = jnp.bfloat16, jnp.float32
VM = pl.BlockSpec(memory_space=pltpu.VMEM)
SM = pl.BlockSpec(memory_space=pltpu.SMEM)
HB = pl.BlockSpec(memory_space=pl.ANY)


def dot_nt(a, b):
    return lax.dot_general(a, b, (((1,), (1,)), ((), ())), preferred_element_type=F32)


def dot_nn(a, b):
    return lax.dot_general(a, b, (((1,), (0,)), ((), ())), preferred_element_type=F32)


def dot_tn(a, b):
    return lax.dot_general(a, b, (((0,), (0,)), ((), ())), preferred_element_type=F32)


def span_ends(where, seg_blocks, seg_audio):
    blocks = [i * NZ * NC + where[1] * NC + where[2] for i in range(NY)]

    def step(s, carry):
        start, found = carry
        end = start + seg_blocks[s]
        value = jnp.where(seg_audio[s] == 1, end * BLK, 0)
        found = tuple(
            jnp.where((start <= b) & (b < end), value, f) for b, f in zip(blocks, found)
        )
        return (end, found)

    zero = jnp.int32(0)
    return lax.fori_loop(0, NSEG, step, (zero, (zero,) * NY))[1]


def pick(i, values):
    out = values[0]
    for n in range(1, len(values)):
        out = jnp.where(i == n, values[n], out)
    return out


def place():
    return tuple(lax.axis_index(name).astype(jnp.int32) for name in ("y", "z", "c", "x"))


def load_all(where, q_refs, o_refs, z_ref, c_ref, q_buf, o_buf, kv_buf, sem):
    y, _, c, x = where
    for r in range(NX):
        j = lax.rem(x + NX - r, NX)
        for e, ref in enumerate((z_ref, c_ref)):
            for d in range(NZ):
                block = d * NC + (c if e == 0 else 1 - c)
                pltpu.make_async_copy(
                    ref.at[d, r], kv_buf.at[:, j, block], sem.at[NY + j]
                ).start()
    for d in range(NY):
        i = lax.rem(y + d, NY)
        pltpu.make_async_copy(q_refs[d], q_buf.at[i], sem.at[i]).start()
        pltpu.make_async_copy(o_refs[d], o_buf.at[i], sem.at[i]).start()


def wait_for(i, q_buf, o_buf, kv_buf, sem):
    pltpu.make_async_copy(q_buf.at[i], q_buf.at[i], sem.at[i]).wait()
    pltpu.make_async_copy(o_buf.at[i], o_buf.at[i], sem.at[i]).wait()
    pltpu.make_async_copy(kv_buf.at[:, i], kv_buf.at[:, i], sem.at[NY + i]).wait()


def visible(where, ends, j, i, count, rows_from, rows):
    n = lax.broadcasted_iota(jnp.int32, (count, 1), 0)
    key_pos = (j * NZ * NC + n // SLICE) * BLK + where[0] * SLICE + n % SLICE
    r = lax.broadcasted_iota(jnp.int32, (1, rows), 1) + rows_from
    query_pos = (i * NZ * NC + where[1] * NC + where[2]) * BLK + r // GROUP
    return key_pos < jnp.maximum(query_pos + 1, pick(i, ends))


def each_pair(ends, pair, ready):
    def full(p, carry):
        i = 1 + (p >= 1).astype(jnp.int32) + (p >= 3).astype(jnp.int32)
        pair(p - i * (i - 1) // 2, i, COL, False, False)
        return carry

    def diagonal(i, carry):
        ready(i)
        pair(i, i, COL, True, True)
        return carry

    def crossing(i, carry):
        @pl.when(pick(i, ends) > (i + 1) * NZ * NC * BLK)
        def _():
            pair(i + 1, i, CROSS, True, False)

        return carry

    lax.fori_loop(0, NY, diagonal, 0)
    lax.fori_loop(0, NY * (NY - 1) // 2, full, 0)
    lax.fori_loop(0, NY - 1, crossing, 0)


def stats_kernel(seg_blocks, seg_audio, *refs):
    q_refs, o_refs = refs[:NY], refs[NY : 2 * NY]
    z_ref, c_ref, out, q_buf, o_buf, kv_buf, high, total, weighted, sem = refs[2 * NY :]
    where = place()
    load_all(where, q_refs, o_refs, z_ref, c_ref, q_buf, o_buf, kv_buf, sem)
    ends = span_ends(where, seg_blocks, seg_audio)
    high[...] = jnp.full_like(high, NEG)
    total[...] = jnp.zeros_like(total)
    weighted[...] = jnp.zeros_like(weighted)

    def pair(j, i, count, masked, first):
        k = kv_buf[0, j].reshape(COL, DH)[:count]
        v = kv_buf[1, j].reshape(COL, DH)[:count]
        for r in range(0, ROWS, RB):
            rows = slice(r, r + RB)
            s = dot_nt(k, q_buf[i, rows, :]) * SCALE2
            if masked:
                seen = visible(where, ends, j, i, count, r, RB)
                s = jnp.where(seen, s, NEG)
            dp = dot_nt(v, o_buf[i, rows, :]).reshape(count // 8, 8, RB)
            s = s.reshape(count // 8, 8, RB)
            old = high[i, :, rows]
            new = jnp.maximum(old, jnp.max(s, axis=0))
            fix = jnp.exp2(old - new)
            p = jnp.exp2(s - new[None])
            if masked:
                p = jnp.where(seen.reshape(count // 8, 8, RB), p, 0.0)
            high[i, :, rows] = new
            total[i, :, rows] = total[i, :, rows] * fix + jnp.sum(p, axis=0)
            weighted[i, :, rows] = weighted[i, :, rows] * fix + jnp.sum(p * dp, axis=0)

    each_pair(ends, pair, lambda i: wait_for(i, q_buf, o_buf, kv_buf, sem))
    top = jnp.max(high[...], axis=1, keepdims=True)
    fix = jnp.exp2(high[...] - top)
    out[:, 0:1, :] = top
    out[:, 1:2, :] = jnp.sum(total[...] * fix, axis=1, keepdims=True)
    out[:, 2:3, :] = jnp.sum(weighted[...] * fix, axis=1, keepdims=True)


def grad_kernel(seg_blocks, seg_audio, *refs):
    q_refs, o_refs, st_refs = refs[:NY], refs[NY : 2 * NY], refs[2 * NY : 3 * NY]
    z_ref, c_ref = refs[3 * NY : 3 * NY + 2]
    dq_outs, (own_out, other_out) = refs[3 * NY + 2 : 4 * NY + 2], refs[4 * NY + 2 : 4 * NY + 4]
    q_buf, o_buf, kv_buf, st_buf, lse, delta, dq, dk, dv, sem, st_sem = refs[4 * NY + 4 :]
    for d in range(NY):
        pltpu.make_async_copy(st_refs[d], st_buf.at[d], st_sem.at[0]).start()
    where = place()
    load_all(where, q_refs, o_refs, z_ref, c_ref, q_buf, o_buf, kv_buf, sem)
    ends = span_ends(where, seg_blocks, seg_audio)
    pltpu.make_async_copy(st_buf, st_buf, st_sem.at[0]).wait()
    top = jnp.max(st_buf[:, :, 0:1, :], axis=0)
    fix = jnp.exp2(st_buf[:, :, 0:1, :] - top[None])
    total = jnp.sum(fix * st_buf[:, :, 1:2, :], axis=0)
    lse[...] = top + jnp.log2(total)
    delta[...] = jnp.sum(fix * st_buf[:, :, 2:3, :], axis=0) / total

    def pair(j, i, count, masked, first):
        k = kv_buf[0, j].reshape(COL, DH)[:count]
        v = kv_buf[1, j].reshape(COL, DH)[:count]
        p_parts, ds_parts = [], []
        for r in range(0, ROWS, RB):
            rows = slice(r, r + RB)
            s = dot_nt(k, q_buf[i, rows, :]) * SCALE2
            p = jnp.exp2(s - lse[i, :, rows])
            if masked:
                p = jnp.where(visible(where, ends, j, i, count, r, RB), p, 0.0)
            dp = dot_nt(v, o_buf[i, rows, :])
            ds = (p * (dp - delta[i, :, rows])).astype(BF)
            if first:
                dq[i, :, rows] = dot_tn(k, ds)
            else:
                dq[i, :, rows] += dot_tn(k, ds)
            p_parts.append(p.astype(BF))
            ds_parts.append(ds)
        dv_part = dot_nn(jnp.concatenate(p_parts, axis=1), o_buf[i])
        dk_part = dot_nn(jnp.concatenate(ds_parts, axis=1), q_buf[i])
        if first:
            dv[j, :count, :] = dv_part
            dk[j, :count, :] = dk_part
        else:
            dv[j, :count, :] += dv_part
            dk[j, :count, :] += dk_part

    each_pair(ends, pair, lambda i: wait_for(i, q_buf, o_buf, kv_buf, sem))
    y, z, c, x = where
    for d in range(NY):
        dq_outs[d][...] = (dq[lax.rem(y + d, NY)].T * SCALE).astype(BF)
    for d in range(NZ):
        first = lax.rem(z + d, NZ) * NC
        for r in range(NX):
            j = lax.rem(x + NX - r, NX)
            for block, out in ((first + c, own_out), (first + 1 - c, other_out)):
                rows = pl.ds(pl.multiple_of(block * SLICE, SLICE), SLICE)
                out[d, r, 0] = dk[j, rows, :] * SCALE
                out[d, r, 1] = dv[j, rows, :]


def buffers():
    return [
        pltpu.VMEM((NY, ROWS, DH), BF),
        pltpu.VMEM((NY, ROWS, DH), BF),
        pltpu.VMEM((2, NY, NZ * NC, SLICE, DH), BF),
    ]


def spread_kernel(b0, b1, b2, b3, key_out, value_out, wide):
    y = lax.axis_index("y").astype(jnp.int32)
    parts = [ref[...].astype(F32) for ref in (b0, b1, b2, b3)]
    for h in range(NX):
        piece = pick(lax.rem(h + NY - y, NX), parts)
        for n in range(2):
            wide[n, :, h, :] = piece[n]
    key_out[...] = wide[0].astype(BF)
    value_out[...] = wide[1].astype(BF)


def spread_call(back):
    out = jax.ShapeDtypeStruct((SLICE, NX, DH), BF)
    return pl.pallas_call(
        spread_kernel,
        out_shape=(out, out),
        in_specs=[VM] * NX,
        out_specs=(VM, VM),
        scratch_shapes=[pltpu.VMEM((2, SLICE, NX, DH), F32)],
        compiler_params=pltpu.CompilerParams(vmem_limit_bytes=4 << 20),
        name="spread",
    )(*map(near, back))


def near(value):
    return pltpu.with_memory_space_constraint(value, pltpu.VMEM)


def stats_call(seg_blocks, seg_audio, q, o, z_all, c_all):
    return pl.pallas_call(
        stats_kernel,
        out_shape=pltpu.VMEM((NY, 3, ROWS), F32),
        in_specs=[SM] * 2 + [HB] * (2 * NY + 2),
        out_specs=VM,
        scratch_shapes=buffers()
        + [pltpu.VMEM((NY, 8, ROWS), F32)] * 3
        + [pltpu.SemaphoreType.DMA((2 * NY,))],
        compiler_params=pltpu.CompilerParams(vmem_limit_bytes=24 << 20),
        name="stats",
    )(seg_blocks, seg_audio, *map(near, (*q, *o, z_all, c_all)))


def grad_call(seg_blocks, seg_audio, q, o, st, z_all, c_all):
    part = pltpu.VMEM((NZ, NX, 2, SLICE, DH), F32)
    return pl.pallas_call(
        grad_kernel,
        out_shape=(pltpu.VMEM((ROWS, DH), BF),) * NY + (part, part),
        in_specs=[SM] * 2 + [HB] * (3 * NY + 2),
        out_specs=(VM,) * (NY + 2),
        scratch_shapes=buffers()
        + [
            pltpu.VMEM((NY, NY, 3, ROWS), F32),
            pltpu.VMEM((NY, 1, ROWS), F32),
            pltpu.VMEM((NY, 1, ROWS), F32),
            pltpu.VMEM((NY, DH, ROWS), F32),
            pltpu.VMEM((NY, COL, DH), F32),
            pltpu.VMEM((NY, COL, DH), F32),
            pltpu.SemaphoreType.DMA((2 * NY,)),
            pltpu.SemaphoreType.DMA((1,)),
        ],
        compiler_params=pltpu.CompilerParams(vmem_limit_bytes=24 << 20),
        name="grads",
    )(seg_blocks, seg_audio, *map(near, (*q, *o, *st, z_all, c_all)))


def shift(value, axis, size, by):
    return lax.ppermute(value, axis, [((n + by) % size, n) for n in range(size)])


def steps(query, key, value, d_out, seg_blocks, seg_audio):
    y, _, _, _ = (lax.axis_index(name).astype(jnp.int32) for name in ("y", "z", "c", "x"))
    heads = jnp.stack([key, value]).transpose(2, 0, 1, 3)
    rounds = []
    for r in range(NX):
        piece = lax.dynamic_index_in_dim(heads, (y + r) % NX, 0, keepdims=False)
        perm = [
            (b * NX + a, a * NX + (b + r) % NX) for b in range(NY) for a in range(NX)
        ]
        rounds.append(lax.ppermute(piece, ("y", "x"), perm))
    own = jnp.stack(rounds)
    q0, o0 = query.reshape(ROWS, DH), d_out.reshape(ROWS, DH)
    q1, q3 = shift(q0, "y", NY, 1), shift(q0, "y", NY, -1)
    o1, o3 = shift(o0, "y", NY, 1), shift(o0, "y", NY, -1)
    q2, o2 = shift(q1, "y", NY, 1), shift(o3, "y", NY, -1)
    z_all = lax.all_to_all(jnp.broadcast_to(own[None], (NZ,) + own.shape), "z", 0, 0)
    c_all = shift(z_all, "c", NC, 1)
    q, o = (q0, q1, q2, q3), (o0, o1, o2, o3)
    st = stats_call(seg_blocks, seg_audio, q, o, z_all, c_all)
    sts = (st,) + tuple(shift(st, "y", NY, d) for d in range(1, NY))
    *dq, own_part, other_part = grad_call(
        seg_blocks, seg_audio, q, o, sts, z_all, c_all
    )
    dq_parts = [shift(dq[d], "y", NY, -d) for d in range(1, NY)]
    dq_sum = dq[0].astype(F32)
    for part in dq_parts:
        dq_sum = dq_sum + part.astype(F32)
    d_query = dq_sum.astype(BF).reshape(BLK, GROUP, DH)
    both = own_part + shift(other_part, "c", NC, 1)
    low = both.astype(BF)
    carried = shift(low[4], "z", NZ, -1)
    third = (both[3] + carried.astype(F32)).astype(BF)
    kv_sum = both[0] + shift(third, "z", NZ, -3).astype(F32)
    for d in (1, 2, 5, 6, 7):
        kv_sum = kv_sum + shift(low[d], "z", NZ, -d).astype(F32)
    kv_low = kv_sum.astype(BF)
    back = []
    for r in range(NX):
        perm = [
            (a * NX + (b + r) % NX, b * NX + a) for b in range(NY) for a in range(NX)
        ]
        back.append(lax.ppermute(kv_low[r], ("y", "x"), perm))
    d_key, d_value = spread_call(back)
    return (d_query, d_key, d_value)


def solution(mesh):
    fine = Mesh(mesh.devices.reshape(NY, NZ, NC, NX), ("y", "z", "c", "x"))
    ctx = ("y", "z", "c")
    rows, tokens = P(ctx, "x", None), P(("y", "z", "c", "x"), None, None)
    return jax.shard_map(
        steps,
        mesh=fine,
        in_specs=(rows, tokens, tokens, rows, P(), P()),
        out_specs=(rows, tokens, tokens),
        check_vma=False,
    )
```
